512 devices in a mesh: blk: 64 (over z, x, core), tp: 8 (over y).
Axes of the slice: x: 4, y: 8, z: 8, core: 2. Of those that a mesh axis runs over, the one named last changes fastest.
Arguments:
- q_new: bfloat16 [4, 512, 4096], P(None, 'blk', 'tp'), may hold values from -48 to 48
- k_new: bfloat16 [4, 512, 1024], P(None, 'blk', 'tp'), may hold values from -4 to 4
- v_new: bfloat16 [4, 512, 1024], P(None, 'blk', 'tp'), may hold values from -6 to 6
- pool_k: bfloat16 [2048, 128, 1024], P('blk', None, 'tp'), may hold values from -6 to 6
- pool_v: bfloat16 [2048, 128, 1024], P('blk', None, 'tp'), may hold values from -6 to 6
- lengths: int32 [512], P('blk'), may hold values from 1 to 508
- table: int32 [512, 4], P('blk'), may hold values from 0 to 31, as said below
- mig_slot: int32 [4], replicated, may hold values from 0 to 7
- mig_dist: int32 [4], replicated, may hold values from 1 to 8
Outputs:
- attn: bfloat16 [4, 512, 4096], P(None, ('blk', 'tp'))
- final_k: bfloat16 [2048, 128, 1024], P('blk', None, 'tp')
- final_v: bfloat16 [2048, 128, 1024], P('blk', None, 'tp')
The draws below stay inside these ranges and needn't reach their ends.
Inputs may be any that keep to these rules, and one draw needn't show every extreme that they name: `table`: on each device the rows of its 8 slots name each of its 32 local pages exactly once.
All inputs are finite; a program needn't handle non-finite values.
Results may differ from the reference program's by a relative error of at most 0.0049.
Values may be sent and summed in bfloat16 or wider, within the bound.
A program may use at most 64 MiB of HBM per device.

```python
import math
import jax
import jax.numpy as jnp
from jax import lax

H = 32
KVH = 8
HD = 128
PAGE = 128
MAXP = 4
STEPS = 4
R_DEV = 8
REQS = 512
POOL_DEV = 32
POOL = 2048
D_MAX = 8


def query_key_pair(key):
    key_query, key_keys = jax.random.split(key, 2)
    query = jnp.clip(jax.random.normal(key_query, (STEPS, REQS, H * HD), jnp.float32), -4.0, 4.0)
    fresh = jnp.clip(jax.random.normal(key_keys, (STEPS, REQS, KVH * HD), jnp.float32), -4.0, 4.0)
    return (query, fresh)


def draw_q_new(key, part):
    query, fresh = query_key_pair(jax.random.fold_in(key, 17))
    return query.astype(jnp.bfloat16)


def draw_k_new(key, part):
    query, fresh = query_key_pair(jax.random.fold_in(key, 17))
    return fresh.astype(jnp.bfloat16)


def draw_table(key, part):
    devices = REQS // R_DEV
    keys_all = jax.random.split(key, devices)
    orders = jax.vmap(lambda single: jax.random.permutation(single, R_DEV * MAXP))(keys_all)
    return orders.reshape(REQS, MAXP).astype(jnp.int32)


def draw_lengths(key, part):
    key_len, key_pos = jax.random.split(key)
    longest = MAXP * PAGE - STEPS
    counts = jax.random.randint(key_len, (REQS,), 1, longest + 1).astype(jnp.int32)
    order = jax.random.permutation(key_pos, REQS)
    counts = counts.at[order[0]].set(longest)
    counts = counts.at[order[1]].set(1)
    return counts


def draw_mig_dist(key, part):
    key_val, key_pos = jax.random.split(key)
    values = jax.random.randint(key_val, (STEPS,), 1, D_MAX + 1).astype(jnp.int32)
    order = jax.random.permutation(key_pos, STEPS)
    values = values.at[order[0]].set(D_MAX)
    values = values.at[order[1]].set(1)
    return values


def with_ends(array, rng, smallest, high):
    extent = array.shape
    spot = [jax.random.randint(jax.random.fold_in(rng, axis), (), 0, extent[axis]) for axis in range(len(extent))]
    array = array.at[tuple(spot)].set(smallest)
    longest = extent.index(max(extent))
    spot[longest] = (spot[longest] + 1) % extent[longest]
    return array.at[tuple(spot)].set(high)


def levels(stream_key, dims, shards, low, largest):
    def one(dim, blocks):
        draws = jax.random.uniform(jax.random.fold_in(jax.random.fold_in(stream_key, 6), dim), (blocks,), jnp.float32, low / len(shards), largest / len(shards))
        return jnp.repeat(jnp.exp(draws), dims[dim] // blocks).reshape((-1,) + (1,) * (len(dims) - dim - 1))

    loudness = one(*shards[0])
    for cut in shards[1:]:
        loudness = loudness * one(*cut)
    return loudness


def scatter_about(rng, extent, scale, most, shards=(), held_as=jnp.bfloat16):
    gain = levels(rng, extent, shards, -0.22, 0.18) if shards else 1.0
    entries = jax.random.normal(rng, extent, jnp.float32) * scale * gain
    return jnp.minimum(jnp.maximum(entries, -most), most).astype(held_as)


def setup_inputs(seed: int = 0) -> dict:
    key_of = jax.random.split(jax.random.key(seed), 10)
    return {
        "q_new": draw_q_new(jax.random.fold_in(key_of[9], 71), 0),
        "k_new": draw_k_new(jax.random.fold_in(key_of[9], 71), 0),
        "v_new": scatter_about(key_of[2], (STEPS, REQS, KVH * HD), 1.0, 6.0, ((1, 64), (2, 8))),
        "pool_k": scatter_about(key_of[3], (POOL, PAGE, KVH * HD), 1.0, 6.0, ((0, 64), (2, 8))),
        "pool_v": scatter_about(key_of[4], (POOL, PAGE, KVH * HD), 1.0, 6.0, ((0, 64), (2, 8))),
        "lengths": draw_lengths(jax.random.fold_in(key_of[9], 71), 0),
        "table": draw_table(jax.random.fold_in(key_of[9], 71), 0),
        "mig_slot": with_ends(jax.random.randint(key_of[7], (STEPS,), 0, R_DEV), jax.random.fold_in(key_of[7], 1), 0, R_DEV - 1).astype(jnp.int32),
        "mig_dist": draw_mig_dist(jax.random.fold_in(key_of[9], 71), 0),
    }


def reference(q_new, k_new, v_new, pool_k, pool_v, lengths, table, mig_slot, mig_dist):
    blocks = REQS // R_DEV
    owner = jnp.arange(REQS, dtype=jnp.int32) // R_DEV * POOL_DEV
    gpage = table + owner[:, None]
    span = MAXP * PAGE
    group = H // KVH
    scale = 1.0 / math.sqrt(HD)
    lens = lengths
    results = []
    for step in range(STEPS):
        position = lens
        page_ids = jnp.take_along_axis(gpage, (position // PAGE)[:, None], axis=1)[:, 0]
        offset = position % PAGE
        pool_k = pool_k.at[page_ids, offset].set(k_new[step])
        pool_v = pool_v.at[page_ids, offset].set(v_new[step])
        lens = lens + 1
        query_all = q_new[step]

        def one_block(index):
            start = index * R_DEV
            pages = lax.dynamic_slice_in_dim(gpage, start, R_DEV, 0)
            count = lax.dynamic_slice_in_dim(lens, start, R_DEV, 0)
            query = lax.dynamic_slice_in_dim(query_all, start, R_DEV, 0)
            query = query.astype(jnp.float32).reshape(R_DEV, KVH, group, HD)
            cached_keys = pool_k[pages].astype(jnp.float32).reshape(R_DEV, span, KVH, HD)
            cached_values = pool_v[pages].astype(jnp.float32).reshape(R_DEV, span, KVH, HD)
            scores = jnp.einsum('rkgd,rlkd->rkgl', query, cached_keys) * scale
            live = jnp.arange(span, dtype=jnp.int32)[None, :] < count[:, None]
            scores = jnp.where(live[:, None, None, :], scores, -jnp.inf)
            top = lax.optimization_barrier(jnp.max(scores, axis=-1, keepdims=True))
            expo = jnp.exp(scores - top)
            weights = (expo / lax.optimization_barrier(jnp.sum(expo, axis=-1, keepdims=True))).astype(jnp.bfloat16)
            weights = lax.optimization_barrier(weights).astype(jnp.float32)
            mixed = jnp.einsum('rkgl,rlkd->rkgd', weights, cached_values)
            return mixed.astype(jnp.bfloat16).reshape(R_DEV, H * HD)
        result = lax.map(one_block, jnp.arange(blocks, dtype=jnp.int32))
        results.append(result.reshape(REQS, H * HD))
        slot = mig_slot[step]
        distance = mig_dist[step]
        column = jnp.arange(blocks, dtype=jnp.int32) * R_DEV + slot
        moving = gpage[column]
        source = (jnp.arange(blocks, dtype=jnp.int32) - distance) % blocks
        pool_k = pool_k.at[moving].set(pool_k[moving][source])
        pool_v = pool_v.at[moving].set(pool_v[moving][source])
        lens = lens.at[column].set(lens[column][source])
    return (jnp.stack(results), pool_k, pool_v)
```

```python
import functools
import math

import jax
import jax.numpy as jnp
from jax import lax
from jax.experimental import pallas as pl
from jax.experimental.pallas import tpu as pltpu
from jax.sharding import PartitionSpec as P

HD = 128
STEPS = 4


def shifted(payload, axis, by):
    size = lax.axis_size(axis)
    return lax.ppermute(payload, axis, [(i, (i + by) % size) for i in range(size)])


def step_kernel(has_prev, table, counts, slots, q_ref, knew_ref, vnew_ref, recv_ref,
                pk_hbm, pv_hbm, attn_ref, pay_ref, pk_out, pv_out, kbuf, vbuf, sems):
    rows, pages = table.shape
    page_len, width = kbuf.shape[1], kbuf.shape[2]
    kv_local = width // HD
    heads = q_ref.shape[1]
    group = heads // kv_local
    span = pages * page_len
    load_k = pltpu.make_async_copy(pk_hbm, kbuf, sems.at[0])
    load_v = pltpu.make_async_copy(pv_hbm, vbuf, sems.at[1])
    load_k.start()
    load_v.start()
    load_k.wait()
    load_v.wait()
    if has_prev:
        came = slots[0]
        for p in range(pages):
            page = table[came, p]
            kbuf[page] = recv_ref[0, p]
            vbuf[page] = recv_ref[1, p]
    row_ids = lax.broadcasted_iota(jnp.int32, (page_len, width), 0)
    for r in range(rows):
        pos = counts[r]
        page = table[r, pos // page_len]
        hit = row_ids == pos % page_len
        kbuf[page] = jnp.where(hit, jnp.broadcast_to(knew_ref[pl.ds(r, 1), :], (page_len, width)), kbuf[page])
        vbuf[page] = jnp.where(hit, jnp.broadcast_to(vnew_ref[pl.ds(r, 1), :], (page_len, width)), vbuf[page])
    going = slots[1]
    for p in range(pages):
        page = table[going, p]
        pay_ref[0, p] = kbuf[page]
        pay_ref[1, p] = vbuf[page]
    store_k = pltpu.make_async_copy(kbuf, pk_out, sems.at[2])
    store_v = pltpu.make_async_copy(vbuf, pv_out, sems.at[3])
    store_k.start()
    store_v.start()
    token_ids = lax.broadcasted_iota(jnp.int32, (group, span), 1)
    scale = 1.0 / math.sqrt(HD)
    for r in range(rows):
        live = token_ids < counts[r] + 1
        ids = [table[r, p] for p in range(pages)]
        outs = []
        for h in range(kv_local):
            lanes = slice(h * HD, (h + 1) * HD)
            query = q_ref[r, h * group:(h + 1) * group, :]
            parts = [
                lax.dot_general(query, kbuf[ids[p]][:, lanes], (((1,), (1,)), ((), ())),
                                preferred_element_type=jnp.float32)
                for p in range(pages)
            ]
            scores = jnp.concatenate(parts, axis=1) * scale
            scores = jnp.where(live, scores, -jnp.inf)
            top = jnp.max(scores, axis=-1, keepdims=True)
            expo = jnp.exp(scores - top)
            weights = (expo / jnp.sum(expo, axis=-1, keepdims=True)).astype(jnp.bfloat16)
            mixed = None
            for p in range(pages):
                term = jnp.dot(weights[:, p * page_len:(p + 1) * page_len], vbuf[ids[p]][:, lanes],
                               preferred_element_type=jnp.float32)
                mixed = term if mixed is None else mixed + term
            outs.append(mixed.astype(jnp.bfloat16))
        attn_ref[r] = jnp.concatenate(outs, axis=0) if kv_local > 1 else outs[0]
    store_k.wait()
    store_v.wait()


def run_step(has_prev, table, counts, slots, query, k_row, v_row, recv, pool_k, pool_v):
    rows, pages = table.shape
    page_len, width = pool_k.shape[1], pool_k.shape[2]
    heads = query.shape[1] // HD
    smem = pl.BlockSpec(memory_space=pltpu.SMEM)
    vmem = pl.BlockSpec(memory_space=pltpu.VMEM)
    anywhere = pl.BlockSpec(memory_space=pl.ANY)
    pool_bytes = pool_k.size * pool_k.dtype.itemsize
    return pl.pallas_call(
        functools.partial(step_kernel, has_prev),
        out_shape=(
            jax.ShapeDtypeStruct((rows, heads, HD), jnp.bfloat16),
            jax.ShapeDtypeStruct((2, pages, page_len, width), pool_k.dtype),
            jax.ShapeDtypeStruct(pool_k.shape, pool_k.dtype),
            jax.ShapeDtypeStruct(pool_v.shape, pool_v.dtype),
        ),
        in_specs=[smem, smem, smem, vmem, vmem, vmem, vmem, anywhere, anywhere],
        out_specs=(vmem, vmem, anywhere, anywhere),
        scratch_shapes=[
            pltpu.VMEM(pool_k.shape, pool_k.dtype),
            pltpu.VMEM(pool_v.shape, pool_v.dtype),
            pltpu.SemaphoreType.DMA((4,)),
        ],
        input_output_aliases={7: 2, 8: 3},
        cost_estimate=pl.CostEstimate(
            flops=4 * rows * heads * pages * page_len * HD,
            transcendentals=rows * heads * pages * page_len,
            bytes_accessed=4 * pool_bytes,
        ),
    )(table, counts, slots, query.reshape(rows, heads, HD), k_row, v_row, recv, pool_k, pool_v)


def local(q_new, k_new, v_new, pool_k, pool_v, lengths, table, mig_slot, mig_dist):
    reach = max(lax.axis_size("blk") // 8, 4)
    rows, pages = table.shape
    page_len, width = pool_k.shape[1], pool_k.shape[2]
    branches = [functools.partial(shifted, axis="blk", by=d) for d in range(1, reach + 1)]
    counts = lengths
    recv = jnp.zeros((2, pages, page_len, width), pool_k.dtype)
    results = []
    for step in range(STEPS):
        came = mig_slot[step - 1] if step else mig_slot[0]
        slots = jnp.stack([came, mig_slot[step]]).astype(jnp.int32)
        attn, payload, pool_k, pool_v = run_step(
            step > 0, table, counts, slots, q_new[step], k_new[step], v_new[step], recv, pool_k, pool_v
        )
        results.append(attn.reshape(rows, -1))
        counts = counts + 1
        slot = mig_slot[step]
        recv, moved = lax.switch(
            jnp.clip(mig_dist[step] - 1, 0, reach - 1),
            branches,
            (payload, lax.dynamic_slice_in_dim(counts, slot, 1)),
        )
        counts = lax.dynamic_update_slice_in_dim(counts, moved, slot, 0)
    last = jnp.take(table, mig_slot[STEPS - 1], axis=0)
    pool_k = pool_k.at[last].set(recv[0], unique_indices=True)
    pool_v = pool_v.at[last].set(recv[1], unique_indices=True)
    stacked = jnp.stack(results)
    attention = lax.all_to_all(stacked, "tp", split_axis=1, concat_axis=2, tiled=True)
    return (attention, pool_k, pool_v)


def solution(mesh):
    placed = (
        P(None, "blk", "tp"),
        P(None, "blk", "tp"),
        P(None, "blk", "tp"),
        P("blk", None, "tp"),
        P("blk", None, "tp"),
        P("blk"),
        P("blk", None),
        P(),
        P(),
    )
    return jax.shard_map(
        local,
        mesh=mesh,
        in_specs=placed,
        out_specs=(P(None, ("blk", "tp"), None), P("blk", None, "tp"), P("blk", None, "tp")),
        check_vma=False,
    )
```
